32 devices in a mesh: gz: 16 (over z, y, core), ta: 2 (over x).
Axes of the slice: x: 2, y: 2, z: 4, core: 2. Of those that a mesh axis runs over, the one named last changes fastest.
Arguments:
- outputs_fwd: bfloat16 [4, 32, 64, 1280], P('ta', 'gz'), may hold values from -6 to 6
- cotangent: bfloat16 [4, 32, 64, 1280], P('ta', 'gz'), may hold values from -6 to 6
- spatial_weight: bfloat16 [3, 64, 288], replicated, may hold values from -0.21875 to 0.21875
- hidden_bias: float32 [64], replicated, may hold values from -1 to 1
- temporal_weight: bfloat16 [3, 32, 64], replicated, may hold values from -0.4375 to 0.4375
Outputs:
- rebuilt: bfloat16 [4, 32, 32, 1280], P('ta', 'gz')
- grad_in: bfloat16 [4, 32, 32, 1280], P('ta', 'gz')
- grad_spatial: float32 [3, 64, 288], replicated
- grad_bias: float32 [64], replicated
- grad_temporal: float32 [3, 32, 64], replicated
The draws below stay inside these ranges and needn't reach their ends.
All inputs are finite; a program needn't handle non-finite values.
Results may differ from the reference program's by a relative error of at most 0.0075.
Values may be sent and summed in bfloat16 or wider, within the bound.
A program may use at most 64 MiB of HBM per device.

```python
import math
import jax
import jax.numpy as jnp
from jax import lax

CH = 32
HID = 64
ROWS = 8
COLS = 160
NZ = 32
FRAMES = 4


def level_of(stream_key, dims, split, smallest, high):
    def one(axis_at, parts):
        heights = jax.random.uniform(jax.random.fold_in(jax.random.fold_in(stream_key, 6), axis_at), (parts,), jnp.float32, smallest / len(split), high / len(split))
        return jnp.repeat(jnp.exp(heights), dims[axis_at] // parts).reshape((-1,) + (1,) * (len(dims) - axis_at - 1))

    gain = one(*split[0])
    for cut in split[1:]:
        gain = gain * one(*cut)
    return gain


def bell_draw(stream_key, dims, scale, bound, split=(), kind=jnp.bfloat16):
    drawn = jax.random.normal(stream_key, dims, jnp.float32) * scale
    if len(split) > 0:
        drawn = level_of(stream_key, dims, split, -0.22, 0.18) * drawn
    return jnp.clip(drawn, min=-bound, max=bound).astype(kind)


def setup_inputs(seed: int = 0) -> dict:
    splits = jax.random.split(jax.random.key(seed), 6)
    return {
        "outputs_fwd": bell_draw(splits[0], (FRAMES, NZ, 2 * CH, ROWS * COLS), 1.0, 6.0, ((0, 2), (1, 16))),
        "cotangent": bell_draw(splits[1], (FRAMES, NZ, 2 * CH, ROWS * COLS), 1.0, 6.0, ((0, 2), (1, 16))),
        "spatial_weight": bell_draw(splits[2], (3, HID, 9 * CH), (27 * CH) ** -0.5, 0.21875),
        "hidden_bias": jnp.clip(jax.random.uniform(splits[3], (HID,), jnp.float32, -1.0, 1.0), -1.0, 1.0),
        "temporal_weight": bell_draw(splits[4], (3, CH, HID), (3 * HID) ** -0.5, 0.4375),
    }


def unfold(field):
    leading = field.shape[:-1]
    planar = field.reshape(leading + (ROWS, COLS))
    padded = jnp.pad(planar, [(0, 0)] * len(leading) + [(1, 1), (1, 1)])
    windows = [padded[..., row_off:row_off + ROWS, col_off:col_off + COLS] for row_off in range(3) for col_off in range(3)]
    stacked = jnp.stack(windows, axis=-4)
    return stacked.reshape(leading[:-1] + (9 * leading[-1], ROWS * COLS))

def linear_frame(frame_in, spatial_weight):
    columns = jnp.pad(unfold(frame_in), ((1, 1), (0, 0), (0, 0))).astype(jnp.float32)
    weight = spatial_weight.astype(jnp.float32)
    total = jnp.einsum('oi,zir->zor', weight[0], columns[0:NZ], precision=lax.Precision.HIGHEST)
    total = total + jnp.einsum('oi,zir->zor', weight[1], columns[1:NZ + 1], precision=lax.Precision.HIGHEST)
    total = total + jnp.einsum('oi,zir->zor', weight[2], columns[2:NZ + 2], precision=lax.Precision.HIGHEST)
    return total

def reference(outputs_fwd, cotangent, spatial_weight, hidden_bias, temporal_weight):
    front_half = outputs_fwd[:, :, :CH]
    back_half = outputs_fwd[:, :, CH:]
    grad_front = cotangent[:, :, :CH]
    grad_back = cotangent[:, :, CH:]
    bias_col = hidden_bias.astype(jnp.float32)[None, :, None]

    def activate(frame_in):
        return jax.nn.silu(linear_frame(frame_in, spatial_weight) + bias_col).astype(jnp.bfloat16)
    active = lax.map(activate, front_half)
    tweight = temporal_weight.astype(jnp.float32)

    def frame_step(carry, index):
        spatial_acc, bias_acc, temporal_acc = carry
        near = [active[(index + offset - 1) % FRAMES].astype(jnp.float32) for offset in range(3)]
        mapped = jnp.einsum('oi,zir->zor', tweight[0], near[0], precision=lax.Precision.HIGHEST)
        mapped = mapped + jnp.einsum('oi,zir->zor', tweight[1], near[1], precision=lax.Precision.HIGHEST)
        mapped = mapped + jnp.einsum('oi,zir->zor', tweight[2], near[2], precision=lax.Precision.HIGHEST)
        rebuilt = (back_half[index].astype(jnp.float32) - mapped).astype(jnp.bfloat16)
        grads_near = [grad_back[(index + 1 - offset) % FRAMES].astype(jnp.float32) for offset in range(3)]
        through = jnp.einsum('oi,zor->zir', tweight[0], grads_near[0], precision=lax.Precision.HIGHEST)
        through = through + jnp.einsum('oi,zor->zir', tweight[1], grads_near[1], precision=lax.Precision.HIGHEST)
        through = through + jnp.einsum('oi,zor->zir', tweight[2], grads_near[2], precision=lax.Precision.HIGHEST)
        own_grad = grad_back[index].astype(jnp.float32)
        temporal_acc = temporal_acc + jnp.stack([jnp.einsum('zor,zir->oi', own_grad, near[offset], precision=lax.Precision.HIGHEST) for offset in range(3)])
        frame_in = front_half[index]
        linear_val, pullback = jax.vjp(lambda field: linear_frame(field, spatial_weight), frame_in.astype(jnp.float32))
        hidden_in = linear_val + bias_col
        sigmoid_val = jax.nn.sigmoid(hidden_in)
        hidden_grad = (through * sigmoid_val * (1.0 + hidden_in * (1.0 - sigmoid_val))).astype(jnp.bfloat16)
        grad_value = hidden_grad.astype(jnp.float32)
        columns = jnp.pad(unfold(frame_in), ((1, 1), (0, 0), (0, 0))).astype(jnp.float32)
        spatial_acc = spatial_acc + jnp.stack([jnp.einsum('zor,zir->oi', grad_value, columns[depth:depth + NZ], precision=lax.Precision.HIGHEST) for depth in range(3)])
        bias_acc = bias_acc + lax.optimization_barrier(jnp.sum(grad_value, axis=(0, 2)))
        input_grad = pullback(grad_value)[0]
        grad_in = (grad_front[index].astype(jnp.float32) + input_grad).astype(jnp.bfloat16)
        return ((spatial_acc, bias_acc, temporal_acc), (rebuilt, grad_in))
    start = (jnp.zeros(spatial_weight.shape, jnp.float32), jnp.zeros((HID,), jnp.float32), jnp.zeros(temporal_weight.shape, jnp.float32))
    carry, (rebuilt, grad_in) = lax.scan(frame_step, start, jnp.arange(FRAMES, dtype=jnp.int32))
    factor = 1.0 / math.sqrt(FRAMES * NZ * ROWS * COLS)
    return (rebuilt, grad_in, carry[0] * factor, carry[1] * factor, carry[2] * factor)
```

```python
import functools
import math

import jax
import jax.numpy as jnp
from jax import lax
from jax.experimental import pallas as pl
from jax.experimental.pallas import tpu as pltpu
from jax.sharding import PartitionSpec as P

ROWS = 8
COLS = 160
F32 = jnp.float32
BF16 = jnp.bfloat16


def levels_of(gz_count, ta_count):
    bits = lambda count: [1 << i for i in range(count.bit_length() - 1)]
    gz_bits = [("gz", bit) for bit in bits(gz_count)]
    ta_bits = [("ta", bit) for bit in bits(ta_count)]
    return gz_bits[:1] + ta_bits + gz_bits[1:]


def nn(lhs, rhs):
    return lax.dot_general(lhs, rhs, (((1,), (0,)), ((), ())), preferred_element_type=F32)


def nt(lhs, rhs):
    return lax.dot_general(lhs, rhs, (((1,), (1,)), ((), ())), preferred_element_type=F32)


def tn(lhs, rhs):
    return lax.dot_general(lhs, rhs, (((0,), (0,)), ((), ())), preferred_element_type=F32)


def kernel(
    gz_count, ta_count, factor,
    x_ref, g_ref, wcat_ref, flip_ref, bias_ref, tw_ref,
    rebuilt_ref, gin_ref, gs_ref, gb_ref, gt_ref,
    cols, hcols, g3, yh, slope, act, hgr, parts, mown, msend, mrecv, psend, precv,
    acc, rs0s, rs0r, acc1, rs1s, rs1r, exs, exr, fin,
    ysem_s, ysem_r, gsem_s, gsem_r, msem_s, msem_r, psem_s, psem_r, asem_s, asem_r,
):
    frames, planes = x_ref.shape[0], x_ref.shape[1]
    half = x_ref.shape[2] // 2
    pix = x_ref.shape[3]
    hid = bias_ref.shape[0]
    me_g = lax.axis_index("gz")
    me_t = lax.axis_index("ta")
    has_l = me_g > 0
    has_r = me_g < gz_count - 1
    mesh_id = pl.DeviceIdType.MESH
    ta_r = lax.rem(me_t + 1, ta_count)
    ta_l = lax.rem(me_t + ta_count - 1, ta_count)
    levels = levels_of(gz_count, ta_count)

    def partner(level):
        axis, bit = levels[level]
        at = me_g if axis == "gz" else me_t
        has = lax.rem(at // bit, 2)
        other = at + bit - 2 * bit * has
        dev = (other, me_t) if axis == "gz" else (me_g, other)
        return dev, has

    barrier = pltpu.get_barrier_semaphore()

    def greet(dev):
        pl.semaphore_signal(barrier, inc=1, device_id=dev, device_id_type=mesh_id)

    greet((me_g, ta_r))
    greet((me_g, ta_l))
    for level in range(len(levels)):
        greet(partner(level)[0])

    @pl.when(has_l)
    def _():
        greet((me_g - 1, me_t))

    @pl.when(has_r)
    def _():
        greet((me_g + 1, me_t))

    beside = has_l.astype(jnp.int32) + has_r.astype(jnp.int32)
    pl.semaphore_wait(barrier, 2 + len(levels) + beside)

    def remote(src, dst, ssem, rsem, dev):
        return pltpu.make_async_remote_copy(
            src_ref=src, dst_ref=dst, send_sem=ssem, recv_sem=rsem, device_id=dev, device_id_type=mesh_id
        )

    y_right = remote(x_ref.at[:, planes - 1, 0:half], yh.at[0], ysem_s.at[0], ysem_r.at[0], (me_g + 1, me_t))
    y_left = remote(x_ref.at[:, 0, 0:half], yh.at[1], ysem_s.at[1], ysem_r.at[1], (me_g - 1, me_t))
    g_left = remote(
        g_ref.at[0, :, half : 2 * half], g3.at[frames - 1, :, 0:half], gsem_s.at[0], gsem_r.at[0], (me_g, ta_l)
    )
    g_right = remote(
        g_ref.at[frames - 1, :, half : 2 * half], g3.at[0, :, 2 * half : 3 * half], gsem_s.at[1], gsem_r.at[1], (me_g, ta_r)
    )
    pl.when(has_r)(y_right.start)
    pl.when(has_l)(y_left.start)
    g_left.start()
    g_right.start()

    for s in range(frames):
        for z in range(planes):
            for k in range(3):
                t = s + 1 - k
                if 0 <= t < frames:
                    g3[s, z, k * half : (k + 1) * half, :] = g_ref[t, z, half : 2 * half, :]

    place = lax.broadcasted_iota(jnp.int32, (1, pix), 1)
    column = lax.rem(place, COLS)
    col_ok = {-1: column > 0, 1: column < COLS - 1}
    row_ok = {-1: place >= COLS, 1: place < pix - COLS}

    def unfold(value, store):
        for c in (-1, 0, 1):
            moved = value
            if c != 0:
                moved = jnp.where(col_ok[c], pltpu.roll(value, (-c) % pix, 1), 0.0)
            for r in (-1, 0, 1):
                out = moved
                if r != 0:
                    out = jnp.where(row_ok[r], pltpu.roll(moved, (-r * COLS) % pix, 1), 0.0)
                store(3 * (r + 1) + c + 1, out.astype(BF16))

    window = 9 * half

    def unfold_y(value, t, plane):
        def store(w, out):
            base = plane * window + w * half
            cols[t, base : base + half, :] = out

        unfold(value.astype(F32), store)

    for t in range(frames):
        for z in range(planes):
            unfold_y(x_ref[t, z, 0:half, :], t, z + 1)

    @pl.when(has_l)
    def _():
        y_right.wait_recv()
        for t in range(frames):
            unfold_y(yh[0, t], t, 0)

    @pl.when(jnp.logical_not(has_l))
    def _():
        for t in range(frames):
            cols[t, 0:window, :] = jnp.zeros((window, pix), BF16)

    @pl.when(has_r)
    def _():
        y_left.wait_recv()
        for t in range(frames):
            unfold_y(yh[1, t], t, planes + 1)

    @pl.when(jnp.logical_not(has_r))
    def _():
        for t in range(frames):
            cols[t, (planes + 1) * window : (planes + 2) * window, :] = jnp.zeros((window, pix), BF16)

    wcat = wcat_ref[...]
    tw = tw_ref[...]
    bias = bias_ref[...]
    for t in range(frames):
        for z in range(planes):
            pre = nn(wcat, cols[t, z * window : (z + 3) * window, :]) + bias
            sig = jax.nn.sigmoid(pre)
            active = (pre * sig).astype(BF16)
            slope[t, z] = sig * (1.0 + pre * (1.0 - sig))
            act[t, z] = active
            mown[t, z] = nn(tw, active)
        if t == 0:
            for z in range(planes):
                msend[1, z] = mown[0, z, 2 * half : 3 * half, :].astype(BF16)
        if t == frames - 1:
            for z in range(planes):
                msend[0, z] = mown[t, z, 0:half, :].astype(BF16)
    m_right = remote(msend.at[0], mrecv.at[0], msem_s.at[0], msem_r.at[0], (me_g, ta_r))
    m_left = remote(msend.at[1], mrecv.at[1], msem_s.at[1], msem_r.at[1], (me_g, ta_l))
    m_right.start()
    m_left.start()

    g_left.wait_recv()
    g_right.wait_recv()
    ones = jnp.ones((8, pix), BF16)
    ssum = jnp.zeros((3 * window, hid), F32)
    tsum = jnp.zeros((3 * half, hid), F32)
    bsum = jnp.zeros((8, hid), F32)
    for t in range(frames):
        for z in range(planes):
            around = g3[t, z]
            hgrad = (tn(tw, around) * slope[t, z]).astype(BF16)
            hgr[t, z] = hgrad
            tsum = tsum + nt(around, act[t, z])
            bsum = bsum + nt(ones, hgrad)
            ssum = ssum + nt(cols[t, z * window : (z + 3) * window, :], hgrad)
    lines = acc.shape[0] // 2
    acc[0:lines, 0:hid] = ssum[0:window]
    acc[0:lines, hid : 2 * hid] = ssum[window : 2 * window]
    acc[lines : 2 * lines, 0:hid] = ssum[2 * window : 3 * window]
    acc[lines : lines + 3 * half, hid : 2 * hid] = tsum
    acc[lines + 3 * half : lines + 3 * half + 8, hid : 2 * hid] = bsum
    acc[lines + 3 * half + 8 : 2 * lines, hid : 2 * hid] = jnp.zeros((lines - 3 * half - 8, hid), F32)

    dev0, bit0 = partner(0)
    dev1, bit1 = partner(1)
    short = lines // 2
    rs0 = remote(rs0s, rs0r, asem_s.at[0], asem_r.at[0], dev0)
    rs1 = remote(rs1s, rs1r, asem_s.at[1], asem_r.at[1], dev1)
    quarter = fin.at[pl.ds(pl.multiple_of(bit0 * lines + bit1 * short, 16), short)]
    side = fin.at[pl.ds(pl.multiple_of(bit0 * lines, 16), lines)]
    last = len(levels)
    ag1 = remote(quarter, quarter, asem_s.at[last], asem_r.at[last], dev1)
    ag0 = remote(side, side, asem_s.at[last + 1], asem_r.at[last + 1], dev0)

    def ex(level):
        return remote(
            exs.at[level - 2], exr.at[level - 2], asem_s.at[level], asem_r.at[level], partner(level)[0]
        )

    def step_first():
        rs0s[...] = acc[pl.ds(pl.multiple_of((1 - bit0) * lines, 16), lines), :].astype(BF16)
        rs0.start()

    def step_second():
        rs0.wait_recv()
        acc1[...] = acc[pl.ds(pl.multiple_of(bit0 * lines, 16), lines), :] + rs0r[...].astype(F32)
        rs1s[...] = acc1[pl.ds(pl.multiple_of((1 - bit1) * short, 16), short), :].astype(BF16)
        rs1.start()

    def hand_on(level, value):
        if level < last:
            exs[level - 2] = value.astype(BF16)
            ex(level).start()
        else:
            fin[pl.ds(pl.multiple_of(bit0 * lines + bit1 * short, 16), short), :] = value.astype(BF16)
            ag1.start()

    def step_third():
        rs1.wait_recv()
        hand_on(2, acc1[pl.ds(pl.multiple_of(bit1 * short, 16), short), :] + rs1r[...].astype(F32))

    def step_ex(level):
        ex(level).wait_recv()
        hand_on(level + 1, exs[level - 2].astype(F32) + exr[level - 2].astype(F32))

    def step_gather():
        ag1.wait_recv()
        ag0.start()

    steps = [step_first, step_second, step_third]
    steps += [functools.partial(step_ex, level) for level in range(2, last)]
    steps += [step_gather]

    steps.pop(0)()

    flip = flip_ref[...]

    def p_right(t):
        return remote(psend.at[0, t], precv.at[0, t], psem_s.at[0, t], psem_r.at[0, t], (me_g + 1, me_t))

    def p_left(t):
        return remote(psend.at[1, t], precv.at[1, t], psem_s.at[1, t], psem_r.at[1, t], (me_g - 1, me_t))

    for t in range(frames):
        for z in range(planes):
            at = t * planes + z

            def store(w, out):
                hcols[at, w * hid : (w + 1) * hid, :] = out

            unfold(hgr[t, z].astype(F32), store)
            parts[t, z] = nn(flip, hcols[at])
            if z == 0:
                psend[1, t] = parts[t, z, 0:half, :].astype(BF16)
                pl.when(has_l)(p_left(t).start)
            if z == planes - 1:
                psend[0, t] = parts[t, z, 2 * half : 3 * half, :].astype(BF16)
                pl.when(has_r)(p_right(t).start)
            if len(steps) > 1:
                steps.pop(0)()

    m_right.wait_recv()
    m_left.wait_recv()
    for t in range(frames):
        for z in range(planes):
            total = mown[t, z, half : 2 * half, :]
            total = total + (mown[t - 1, z, 0:half, :] if t > 0 else mrecv[0, z].astype(F32))
            total = total + (mown[t + 1, z, 2 * half : 3 * half, :] if t < frames - 1 else mrecv[1, z].astype(F32))
            rebuilt_ref[t, z] = (x_ref[t, z, half : 2 * half, :].astype(F32) - total).astype(BF16)
    if len(steps) > 1:
        steps.pop(0)()

    @pl.when(has_l)
    def _():
        for t in range(frames):
            p_right(t).wait_recv()

    @pl.when(jnp.logical_not(has_l))
    def _():
        precv[0] = jnp.zeros_like(precv[0])

    @pl.when(has_r)
    def _():
        for t in range(frames):
            p_left(t).wait_recv()

    @pl.when(jnp.logical_not(has_r))
    def _():
        precv[1] = jnp.zeros_like(precv[1])

    for t in range(frames):
        for z in range(planes):
            total = parts[t, z, half : 2 * half, :]
            total = total + (parts[t, z - 1, 2 * half : 3 * half, :] if z > 0 else precv[0, t].astype(F32))
            total = total + (parts[t, z + 1, 0:half, :] if z < planes - 1 else precv[1, t].astype(F32))
            gin_ref[t, z] = (g_ref[t, z, 0:half, :].astype(F32) + total).astype(BF16)

    while steps:
        steps.pop(0)()
    ag0.wait_recv()
    top = fin[0:lines, :].astype(F32) * factor
    turned = top.T
    gs_ref[0] = turned[0:hid]
    gs_ref[1] = turned[hid : 2 * hid]
    low = fin[lines : 2 * lines, :].astype(F32) * factor
    gs_ref[2] = low.T[0:hid]
    for k in range(3):
        gt_ref[k] = low[k * half : (k + 1) * half, hid : 2 * hid]
    gb_ref[...] = low[3 * half : 3 * half + 1, hid : 2 * hid]

    pl.when(has_r)(y_right.wait_send)
    pl.when(has_l)(y_left.wait_send)
    g_left.wait_send()
    g_right.wait_send()
    m_right.wait_send()
    m_left.wait_send()

    @pl.when(has_r)
    def _():
        for t in range(frames):
            p_right(t).wait_send()

    @pl.when(has_l)
    def _():
        for t in range(frames):
            p_left(t).wait_send()

    rs0.wait_send()
    rs1.wait_send()
    for level in range(2, last):
        ex(level).wait_send()
    ag1.wait_send()
    ag0.wait_send()


def shards(gz_count, ta_count, outputs_fwd, cotangent, spatial_weight, hidden_bias, temporal_weight):
    frames, planes, channels, pix = outputs_fwd.shape
    half = channels // 2
    hid = spatial_weight.shape[1]
    window = 9 * half
    wcat = spatial_weight.transpose((1, 0, 2)).reshape((hid, 3 * window))
    flip = (
        spatial_weight.reshape((3, hid, 9, half))[:, :, ::-1]
        .transpose((0, 3, 2, 1))
        .reshape((3 * half, 9 * hid))
    )
    tw = temporal_weight.reshape((3 * half, hid))
    factor = 1.0 / math.sqrt(frames * ta_count * planes * gz_count * ROWS * COLS)
    vmem = pl.BlockSpec(memory_space=pltpu.VMEM)
    lines = window
    count = len(levels_of(gz_count, ta_count))
    dma = pltpu.SemaphoreType.DMA
    field = jax.ShapeDtypeStruct((frames, planes, half, pix), BF16)
    outs = pl.pallas_call(
        functools.partial(kernel, gz_count, ta_count, factor),
        out_shape=(
            field,
            field,
            jax.ShapeDtypeStruct((3, hid, window), F32),
            jax.ShapeDtypeStruct((1, hid), F32),
            jax.ShapeDtypeStruct((3, half, hid), F32),
        ),
        in_specs=[vmem] * 6,
        out_specs=(vmem,) * 5,
        scratch_shapes=[
            pltpu.VMEM((frames, (planes + 2) * window, pix), BF16),
            pltpu.VMEM((frames * planes, 9 * hid, pix), BF16),
            pltpu.VMEM((frames, planes, 3 * half, pix), BF16),
            pltpu.VMEM((2, frames, half, pix), BF16),
            pltpu.VMEM((frames, planes, hid, pix), F32),
            pltpu.VMEM((frames, planes, hid, pix), BF16),
            pltpu.VMEM((frames, planes, hid, pix), BF16),
            pltpu.VMEM((frames, planes, 3 * half, pix), F32),
            pltpu.VMEM((frames, planes, 3 * half, pix), F32),
            pltpu.VMEM((2, planes, half, pix), BF16),
            pltpu.VMEM((2, planes, half, pix), BF16),
            pltpu.VMEM((2, frames, half, pix), BF16),
            pltpu.VMEM((2, frames, half, pix), BF16),
            pltpu.VMEM((2 * lines, 2 * hid), F32),
            pltpu.VMEM((lines, 2 * hid), BF16),
            pltpu.VMEM((lines, 2 * hid), BF16),
            pltpu.VMEM((lines, 2 * hid), F32),
            pltpu.VMEM((lines // 2, 2 * hid), BF16),
            pltpu.VMEM((lines // 2, 2 * hid), BF16),
            pltpu.VMEM((max(count - 2, 1), lines // 2, 2 * hid), BF16),
            pltpu.VMEM((max(count - 2, 1), lines // 2, 2 * hid), BF16),
            pltpu.VMEM((2 * lines, 2 * hid), BF16),
            dma((2,)), dma((2,)), dma((2,)), dma((2,)), dma((2,)), dma((2,)),
            dma((2, frames)), dma((2, frames)), dma((count + 2,)), dma((count + 2,)),
        ],
        compiler_params=pltpu.CompilerParams(
            collective_id=0, has_side_effects=True, vmem_limit_bytes=56 * 1024 * 1024
        ),
    )(outputs_fwd, cotangent, wcat, flip, hidden_bias[:, None], tw)
    return outs[0], outs[1], outs[2], outs[3].reshape((hid,)), outs[4]


def solution(mesh):
    placed = (P("ta", "gz", None, None), P("ta", "gz", None, None), P(), P(), P())
    return jax.shard_map(
        functools.partial(shards, mesh.shape["gz"], mesh.shape["ta"]),
        mesh=mesh,
        in_specs=placed,
        out_specs=(P("ta", "gz", None, None), P("ta", "gz", None, None), P(), P(), P()),
        check_vma=False,
    )
```

```python
import functools
import math

import jax
import jax.numpy as jnp
from jax import lax
from jax.experimental import pallas as pl
from jax.experimental.pallas import tpu as pltpu
from jax.sharding import PartitionSpec as P

ROWS = 8
COLS = 160
F32 = jnp.float32
BF16 = jnp.bfloat16


def groups_of(gz_count, ta_count):
    bits = lambda count: [1 << i for i in range(count.bit_length() - 1)]
    gz_bits = [("gz", bit) for bit in bits(gz_count)]
    ta_bits = [("ta", bit) for bit in bits(ta_count)]
    return gz_bits[:2] + ta_bits[:1], gz_bits[2:] + ta_bits[1:]


def slot_rows(window, cube):
    return -(-2 * window // (16 * cube)) * 16


def nn(lhs, rhs):
    return lax.dot_general(lhs, rhs, (((1,), (0,)), ((), ())), preferred_element_type=F32)


def nt(lhs, rhs):
    return lax.dot_general(lhs, rhs, (((1,), (1,)), ((), ())), preferred_element_type=F32)


def tn(lhs, rhs):
    return lax.dot_general(lhs, rhs, (((0,), (0,)), ((), ())), preferred_element_type=F32)


def kernel(
    gz_count, ta_count,
    x_ref, g_ref, sw_ref, bias_ref, tw_ref,
    rebuilt_ref, gin_ref, fin,
    cols, hcols, g3, yh, slope, act, hgr, parts, mown, msend, mrecv, psend, precv,
    wcat, flip, acc, accb, first, second,
    ysem_s, ysem_r, gsem_s, gsem_r, msem_s, msem_r, psem_s, psem_r,
    asem_s, asem_r, bsem_s, bsem_r, csem_s, csem_r,
):
    frames, planes = x_ref.shape[0], x_ref.shape[1]
    half = x_ref.shape[2] // 2
    pix = x_ref.shape[3]
    hid = bias_ref.shape[1]
    me_g = lax.axis_index("gz")
    me_t = lax.axis_index("ta")
    has_l = me_g > 0
    has_r = me_g < gz_count - 1
    mesh_id = pl.DeviceIdType.MESH
    ta_r = lax.rem(me_t + 1, ta_count)
    ta_l = lax.rem(me_t + ta_count - 1, ta_count)
    near_bits, far_bits = groups_of(gz_count, ta_count)

    def member(group, flip_mask):
        place = {"gz": me_g, "ta": me_t}
        index = 0
        for order, (axis, bit) in enumerate(group):
            at = me_g if axis == "gz" else me_t
            has = lax.rem(at // bit, 2)
            if flip_mask >> order & 1:
                place[axis] = place[axis] + bit - 2 * bit * has
                has = 1 - has
            index = index + (has << order)
        return (place["gz"], place["ta"]), index

    near_count, far_count = 1 << len(near_bits), 1 << len(far_bits)

    barrier = pltpu.get_barrier_semaphore()

    def greet(dev):
        pl.semaphore_signal(barrier, inc=1, device_id=dev, device_id_type=mesh_id)

    greet((me_g, ta_r))
    greet((me_g, ta_l))
    for j in range(1, near_count):
        greet(member(near_bits, j)[0])
    for j in range(1, far_count):
        greet(member(far_bits, j)[0])

    @pl.when(has_l)
    def _():
        greet((me_g - 1, me_t))

    @pl.when(has_r)
    def _():
        greet((me_g + 1, me_t))

    window = 9 * half
    for dz in range(3):
        wcat[:, dz * window : (dz + 1) * window] = sw_ref[dz]
        turned = sw_ref[dz].astype(F32).T.astype(BF16)
        for w in range(9):
            flip[dz * half : (dz + 1) * half, w * hid : (w + 1) * hid] = turned[(8 - w) * half : (9 - w) * half]
    bias = jnp.broadcast_to(bias_ref[...], (8, hid)).T[:, 0:1]
    beside = has_l.astype(jnp.int32) + has_r.astype(jnp.int32)
    pl.semaphore_wait(barrier, near_count + far_count + beside)

    def remote(src, dst, ssem, rsem, dev):
        return pltpu.make_async_remote_copy(
            src_ref=src, dst_ref=dst, send_sem=ssem, recv_sem=rsem, device_id=dev, device_id_type=mesh_id
        )

    y_right = remote(x_ref.at[:, planes - 1, 0:half], yh.at[0], ysem_s.at[0], ysem_r.at[0], (me_g + 1, me_t))
    y_left = remote(x_ref.at[:, 0, 0:half], yh.at[1], ysem_s.at[1], ysem_r.at[1], (me_g - 1, me_t))
    g_left = [
        remote(
            g_ref.at[0, z, half : 2 * half], g3.at[frames - 1, z, 0:half],
            gsem_s.at[0, z], gsem_r.at[0, z], (me_g, ta_l),
        )
        for z in range(planes)
    ]
    g_right = [
        remote(
            g_ref.at[frames - 1, z, half : 2 * half], g3.at[0, z, 2 * half : 3 * half],
            gsem_s.at[1, z], gsem_r.at[1, z], (me_g, ta_r),
        )
        for z in range(planes)
    ]
    pl.when(has_r)(y_right.start)
    pl.when(has_l)(y_left.start)
    for z in range(planes):
        g_left[z].start()
        g_right[z].start()

    for s in range(frames):
        for z in range(planes):
            for k in range(3):
                t = s + 1 - k
                if 0 <= t < frames:
                    g3[s, z, k * half : (k + 1) * half, :] = g_ref[t, z, half : 2 * half, :]

    place = lax.broadcasted_iota(jnp.int32, (1, pix), 1)
    column = lax.rem(place, COLS)
    col_ok = {-1: column > 0, 1: column < COLS - 1}
    row_ok = {-1: place >= COLS, 1: place < pix - COLS}

    def unfold(value, store):
        for c in (-1, 0, 1):
            moved = value
            if c != 0:
                moved = jnp.where(col_ok[c], pltpu.roll(value, (-c) % pix, 1), 0.0)
            for r in (-1, 0, 1):
                out = moved
                if r != 0:
                    out = jnp.where(row_ok[r], pltpu.roll(moved, (-r * COLS) % pix, 1), 0.0)
                store(3 * (r + 1) + c + 1, out.astype(BF16))

    def unfold_y(value, t, plane):
        def store(w, out):
            base = plane * window + w * half
            cols[t, base : base + half, :] = out

        unfold(value.astype(F32), store)

    for t in range(frames):
        for z in range(planes):
            unfold_y(x_ref[t, z, 0:half, :], t, z + 1)

    @pl.when(has_l)
    def _():
        y_right.wait_recv()
        for t in range(frames):
            unfold_y(yh[0, t], t, 0)

    @pl.when(jnp.logical_not(has_l))
    def _():
        for t in range(frames):
            cols[t, 0:window, :] = jnp.zeros((window, pix), BF16)

    @pl.when(has_r)
    def _():
        y_left.wait_recv()
        for t in range(frames):
            unfold_y(yh[1, t], t, planes + 1)

    @pl.when(jnp.logical_not(has_r))
    def _():
        for t in range(frames):
            cols[t, (planes + 1) * window : (planes + 2) * window, :] = jnp.zeros((window, pix), BF16)

    whole = wcat[...]
    tw = tw_ref[...]
    for t in range(frames):
        for z in range(planes):
            pre = nn(whole, cols[t, z * window : (z + 3) * window, :]) + bias
            sig = jax.nn.sigmoid(pre)
            active = (pre * sig).astype(BF16)
            slope[t, z] = sig * (1.0 + pre * (1.0 - sig))
            act[t, z] = active
            mown[t, z] = nn(tw, active)
        if t == 0:
            for z in range(planes):
                msend[1, z] = mown[0, z, 2 * half : 3 * half, :].astype(BF16)
        if t == frames - 1:
            for z in range(planes):
                msend[0, z] = mown[t, z, 0:half, :].astype(BF16)
    m_right = remote(msend.at[0], mrecv.at[0], msem_s.at[0], msem_r.at[0], (me_g, ta_r))
    m_left = remote(msend.at[1], mrecv.at[1], msem_s.at[1], msem_r.at[1], (me_g, ta_l))
    m_right.start()

    ones = jnp.ones((8, pix), BF16)
    ssum = jnp.zeros((3 * window, hid), F32)
    tsum = jnp.zeros((3 * half, hid), F32)
    bsum = jnp.zeros((8, hid), F32)
    for z in range(planes):
        g_left[z].wait_recv()
        g_right[z].wait_recv()
        for t in range(frames):
            around = g3[t, z]
            hgrad = (tn(tw, around) * slope[t, z]).astype(BF16)
            hgr[t, z] = hgrad
            tsum = tsum + nt(around, act[t, z])
            bsum = bsum + nt(ones, hgrad)
            ssum = ssum + nt(cols[t, z * window : (z + 3) * window, :], hgrad)
    acc[0:window, 0:hid] = ssum[0:window]
    acc[0:window, hid : 2 * hid] = ssum[window : 2 * window]
    acc[window : 2 * window, 0:hid] = ssum[2 * window : 3 * window]
    used = window + 3 * half
    acc[window:used, hid : 2 * hid] = tsum
    acc[used : used + 8, hid : 2 * hid] = bsum
    acc[used + 8 : 2 * window, hid : 2 * hid] = jnp.zeros((2 * window - used - 8, hid), F32)
    if acc.shape[0] > 2 * window:
        acc[2 * window :, :] = jnp.zeros((acc.shape[0] - 2 * window, 2 * hid), F32)
    accb[...] = acc[...].astype(BF16)

    rows = acc.shape[0] // near_count

    def span(index):
        return pl.ds(pl.multiple_of(index * rows, 16), rows)

    near_me = member(near_bits, 0)[1]
    far_me = member(far_bits, 0)[1]
    scatter, share, gather = [], [], []
    for j in range(1, near_count):
        dev, index = member(near_bits, j)
        scatter.append(remote(accb.at[span(index)], first.at[j - 1], asem_s.at[j - 1], asem_r.at[j - 1], dev))
        mine = fin.at[span(near_me)]
        gather.append(remote(mine, mine, csem_s.at[j - 1], csem_r.at[j - 1], dev))
    for j in range(1, far_count):
        dev, _ = member(far_bits, j)
        share.append(remote(second.at[far_me], second.at[far_me], bsem_s.at[j - 1], bsem_r.at[j - 1], dev))
    for copy in scatter:
        copy.start()
    m_left.start()

    def step_share():
        total = acc[span(near_me), :]
        for j, copy in enumerate(scatter):
            copy.wait_recv()
            total = total + first[j].astype(F32)
        second[pl.ds(far_me, 1)] = total.astype(BF16)[None]
        for copy in share:
            copy.start()

    def step_gather():
        for copy in share:
            copy.wait_recv()
        total = second[0].astype(F32)
        for j in range(1, far_count):
            total = total + second[j].astype(F32)
        fin[span(near_me), :] = total.astype(BF16)
        for copy in gather:
            copy.start()

    back = flip[...]

    def p_right(t):
        return remote(psend.at[0, t], precv.at[0, t], psem_s.at[0, t], psem_r.at[0, t], (me_g + 1, me_t))

    def p_left(t):
        return remote(psend.at[1, t], precv.at[1, t], psem_s.at[1, t], psem_r.at[1, t], (me_g - 1, me_t))

    for t in range(frames):
        for z in range(planes):
            at = t * planes + z

            def store(w, out):
                hcols[at, w * hid : (w + 1) * hid, :] = out

            unfold(hgr[t, z].astype(F32), store)
            parts[t, z] = nn(back, hcols[at])
            if z == 0:
                psend[1, t] = parts[t, z, 0:half, :].astype(BF16)
                pl.when(has_l)(p_left(t).start)
            if z == planes - 1:
                psend[0, t] = parts[t, z, 2 * half : 3 * half, :].astype(BF16)
                pl.when(has_r)(p_right(t).start)
            if at == max(frames * planes - 2, 0):
                step_share()

    m_right.wait_recv()
    m_left.wait_recv()
    for t in range(frames):
        for z in range(planes):
            total = mown[t, z, half : 2 * half, :]
            total = total + (mown[t - 1, z, 0:half, :] if t > 0 else mrecv[0, z].astype(F32))
            total = total + (mown[t + 1, z, 2 * half : 3 * half, :] if t < frames - 1 else mrecv[1, z].astype(F32))
            rebuilt_ref[t, z] = (x_ref[t, z, half : 2 * half, :].astype(F32) - total).astype(BF16)
    step_gather()

    @pl.when(has_l)
    def _():
        for t in range(frames):
            p_right(t).wait_recv()

    @pl.when(jnp.logical_not(has_l))
    def _():
        precv[0] = jnp.zeros_like(precv[0])

    @pl.when(has_r)
    def _():
        for t in range(frames):
            p_left(t).wait_recv()

    @pl.when(jnp.logical_not(has_r))
    def _():
        precv[1] = jnp.zeros_like(precv[1])

    for t in range(frames):
        for z in range(planes):
            total = parts[t, z, half : 2 * half, :]
            total = total + (parts[t, z - 1, 2 * half : 3 * half, :] if z > 0 else precv[0, t].astype(F32))
            total = total + (parts[t, z + 1, 0:half, :] if z < planes - 1 else precv[1, t].astype(F32))
            gin_ref[t, z] = (g_ref[t, z, 0:half, :].astype(F32) + total).astype(BF16)

    for copy in gather:
        copy.wait_recv()

    pl.when(has_r)(y_right.wait_send)
    pl.when(has_l)(y_left.wait_send)
    for z in range(planes):
        g_left[z].wait_send()
        g_right[z].wait_send()
    m_right.wait_send()
    m_left.wait_send()

    @pl.when(has_r)
    def _():
        for t in range(frames):
            p_right(t).wait_send()

    @pl.when(has_l)
    def _():
        for t in range(frames):
            p_left(t).wait_send()

    for copy in scatter + share + gather:
        copy.wait_send()


def finish(factor, rebuilt_in, gin_in, fin, rebuilt_ref, gin_ref, gs_ref, gb_ref, gt_ref):
    hid, window = gs_ref.shape[1], gs_ref.shape[2]
    half = window // 9
    rebuilt_ref[...] = rebuilt_in[...]
    gin_ref[...] = gin_in[...]
    turned = (fin[0:window, :].astype(F32) * factor).T
    gs_ref[0] = turned[0:hid]
    gs_ref[1] = turned[hid : 2 * hid]
    low = fin[window : 2 * window, :].astype(F32) * factor
    gs_ref[2] = low.T[0:hid]
    for k in range(3):
        gt_ref[k] = low[k * half : (k + 1) * half, hid : 2 * hid]
    gb_ref[...] = low[3 * half : 3 * half + 1, hid : 2 * hid]


def shards(gz_count, ta_count, outputs_fwd, cotangent, spatial_weight, hidden_bias, temporal_weight):
    frames, planes, channels, pix = outputs_fwd.shape
    half = channels // 2
    hid = spatial_weight.shape[1]
    window = 9 * half
    tw = temporal_weight.reshape((3 * half, hid))
    factor = 1.0 / math.sqrt(frames * ta_count * planes * gz_count * ROWS * COLS)
    vmem = pl.BlockSpec(memory_space=pltpu.VMEM)
    near_bits, far_bits = groups_of(gz_count, ta_count)
    near_count, far_count = 1 << len(near_bits), 1 << len(far_bits)
    rows = slot_rows(window, near_count)
    dma = pltpu.SemaphoreType.DMA
    field = jax.ShapeDtypeStruct((frames, planes, half, pix), BF16)
    outs = pl.pallas_call(
        functools.partial(kernel, gz_count, ta_count),
        out_shape=(
            field,
            field,
            jax.ShapeDtypeStruct((near_count * rows, 2 * hid), BF16),
        ),
        in_specs=[vmem] * 5,
        out_specs=(vmem,) * 3,
        scratch_shapes=[
            pltpu.VMEM((frames, (planes + 2) * window, pix), BF16),
            pltpu.VMEM((frames * planes, 9 * hid, pix), BF16),
            pltpu.VMEM((frames, planes, 3 * half, pix), BF16),
            pltpu.VMEM((2, frames, half, pix), BF16),
            pltpu.VMEM((frames, planes, hid, pix), F32),
            pltpu.VMEM((frames, planes, hid, pix), BF16),
            pltpu.VMEM((frames, planes, hid, pix), BF16),
            pltpu.VMEM((frames, planes, 3 * half, pix), F32),
            pltpu.VMEM((frames, planes, 3 * half, pix), F32),
            pltpu.VMEM((2, planes, half, pix), BF16),
            pltpu.VMEM((2, planes, half, pix), BF16),
            pltpu.VMEM((2, frames, half, pix), BF16),
            pltpu.VMEM((2, frames, half, pix), BF16),
            pltpu.VMEM((hid, 3 * window), BF16),
            pltpu.VMEM((3 * half, 9 * hid), BF16),
            pltpu.VMEM((near_count * rows, 2 * hid), F32),
            pltpu.VMEM((near_count * rows, 2 * hid), BF16),
            pltpu.VMEM((near_count - 1, rows, 2 * hid), BF16),
            pltpu.VMEM((far_count, rows, 2 * hid), BF16),
            dma((2,)), dma((2,)), dma((2, planes)), dma((2, planes)), dma((2,)), dma((2,)),
            dma((2, frames)), dma((2, frames)),
            dma((near_count - 1,)), dma((near_count - 1,)),
            dma((far_count - 1,)), dma((far_count - 1,)),
            dma((near_count - 1,)), dma((near_count - 1,)),
        ],
        compiler_params=pltpu.CompilerParams(
            collective_id=0, has_side_effects=True, vmem_limit_bytes=36 * 1024 * 1024
        ),
    )(outputs_fwd, cotangent, spatial_weight, hidden_bias[None, :], tw)
    ends = pl.pallas_call(
        functools.partial(finish, factor),
        out_shape=(
            field,
            field,
            jax.ShapeDtypeStruct((3, hid, window), F32),
            jax.ShapeDtypeStruct((1, hid), F32),
            jax.ShapeDtypeStruct((3, half, hid), F32),
        ),
        in_specs=[vmem] * 3,
        out_specs=(vmem,) * 5,
        compiler_params=pltpu.CompilerParams(vmem_limit_bytes=8 * 1024 * 1024),
    )(*outs)
    return ends[0], ends[1], ends[2], ends[3].reshape((hid,)), ends[4]


def solution(mesh):
    placed = (P("ta", "gz", None, None), P("ta", "gz", None, None), P(), P(), P())
    return jax.shard_map(
        functools.partial(shards, mesh.shape["gz"], mesh.shape["ta"]),
        mesh=mesh,
        in_specs=placed,
        out_specs=(P("ta", "gz", None, None), P("ta", "gz", None, None), P(), P(), P()),
        check_vma=False,
    )
```

```python
import functools
import math

import jax
import jax.numpy as jnp
from jax import lax
from jax.experimental import pallas as pl
from jax.experimental.pallas import tpu as pltpu
from jax.sharding import PartitionSpec as P

ROWS = 8
COLS = 160
F32 = jnp.float32
BF16 = jnp.bfloat16


def groups_of(gz_count, ta_count):
    bits = lambda count: [1 << i for i in range(count.bit_length() - 1)]
    gz_bits = [("gz", bit) for bit in bits(gz_count)]
    ta_bits = [("ta", bit) for bit in bits(ta_count)]
    return gz_bits[:2] + ta_bits[:1], gz_bits[2:] + ta_bits[1:]


def slot_rows(window, cube):
    return -(-2 * window // (16 * cube)) * 16


def nn(lhs, rhs):
    return lax.dot_general(lhs, rhs, (((1,), (0,)), ((), ())), preferred_element_type=F32)


def nt(lhs, rhs):
    return lax.dot_general(lhs, rhs, (((1,), (1,)), ((), ())), preferred_element_type=F32)


def tn(lhs, rhs):
    return lax.dot_general(lhs, rhs, (((0,), (0,)), ((), ())), preferred_element_type=F32)


def kernel(
    gz_count, ta_count,
    x_hbm, g_hbm, sw_hbm, bias_hbm, tw_hbm,
    rebuilt_ref, gin_ref, fin,
    cols, hcols, g3, yh, slope, act, hgr, parts, mown, msend, mrecv, psend, precv,
    x_ref, g_ref, sw_ref, bias_ref, tw_ref, lsem, wcat, flip, acc, accb, first, second,
    ysem_s, ysem_r, gsem_s, gsem_r, msem_s, msem_r, psem_s, psem_r,
    asem_s, asem_r, bsem_s, bsem_r, csem_s, csem_r,
):
    frames, planes = x_ref.shape[0], x_ref.shape[1]
    half = x_ref.shape[2] // 2
    pix = x_ref.shape[3]
    hid = bias_ref.shape[1]
    me_g = lax.axis_index("gz")
    me_t = lax.axis_index("ta")
    has_l = me_g > 0
    has_r = me_g < gz_count - 1
    mesh_id = pl.DeviceIdType.MESH
    ta_r = lax.rem(me_t + 1, ta_count)
    ta_l = lax.rem(me_t + ta_count - 1, ta_count)
    near_bits, far_bits = groups_of(gz_count, ta_count)

    def member(group, flip_mask):
        place = {"gz": me_g, "ta": me_t}
        index = 0
        for order, (axis, bit) in enumerate(group):
            at = me_g if axis == "gz" else me_t
            has = lax.rem(at // bit, 2)
            if flip_mask >> order & 1:
                place[axis] = place[axis] + bit - 2 * bit * has
                has = 1 - has
            index = index + (has << order)
        return (place["gz"], place["ta"]), index

    near_count, far_count = 1 << len(near_bits), 1 << len(far_bits)

    pairs = ((sw_hbm, sw_ref), (bias_hbm, bias_ref), (tw_hbm, tw_ref), (x_hbm, x_ref), (g_hbm, g_ref))
    loads = [pltpu.make_async_copy(src, dst, lsem.at[i]) for i, (src, dst) in enumerate(pairs)]
    barrier = pltpu.get_barrier_semaphore()

    def greet(dev):
        pl.semaphore_signal(barrier, inc=1, device_id=dev, device_id_type=mesh_id)

    greet((me_g, ta_r))
    greet((me_g, ta_l))
    for j in range(1, near_count):
        greet(member(near_bits, j)[0])
    for j in range(1, far_count):
        greet(member(far_bits, j)[0])

    @pl.when(has_l)
    def _():
        greet((me_g - 1, me_t))

    @pl.when(has_r)
    def _():
        greet((me_g + 1, me_t))

    for load in loads:
        load.start()
    for load in loads[:3]:
        load.wait()
    window = 9 * half
    for dz in range(3):
        wcat[:, dz * window : (dz + 1) * window] = sw_ref[dz]
        turned = sw_ref[dz].astype(F32).T.astype(BF16)
        for w in range(9):
            flip[dz * half : (dz + 1) * half, w * hid : (w + 1) * hid] = turned[(8 - w) * half : (9 - w) * half]
    bias = jnp.broadcast_to(bias_ref[...], (8, hid)).T[:, 0:1]
    beside = has_l.astype(jnp.int32) + has_r.astype(jnp.int32)
    pl.semaphore_wait(barrier, near_count + far_count + beside)

    def remote(src, dst, ssem, rsem, dev):
        return pltpu.make_async_remote_copy(
            src_ref=src, dst_ref=dst, send_sem=ssem, recv_sem=rsem, device_id=dev, device_id_type=mesh_id
        )

    y_right = remote(x_hbm.at[:, planes - 1, 0:half], yh.at[0], ysem_s.at[0], ysem_r.at[0], (me_g + 1, me_t))
    y_left = remote(x_hbm.at[:, 0, 0:half], yh.at[1], ysem_s.at[1], ysem_r.at[1], (me_g - 1, me_t))
    g_left = [
        remote(
            g_hbm.at[0, z, half : 2 * half], g3.at[frames - 1, z, 0:half],
            gsem_s.at[0, z], gsem_r.at[0, z], (me_g, ta_l),
        )
        for z in range(planes)
    ]
    g_right = [
        remote(
            g_hbm.at[frames - 1, z, half : 2 * half], g3.at[0, z, 2 * half : 3 * half],
            gsem_s.at[1, z], gsem_r.at[1, z], (me_g, ta_r),
        )
        for z in range(planes)
    ]
    pl.when(has_r)(y_right.start)
    pl.when(has_l)(y_left.start)
    for z in range(planes):
        g_left[z].start()
        g_right[z].start()

    for load in loads[3:]:
        load.wait()
    for s in range(frames):
        for z in range(planes):
            for k in range(3):
                t = s + 1 - k
                if 0 <= t < frames:
                    g3[s, z, k * half : (k + 1) * half, :] = g_ref[t, z, half : 2 * half, :]

    place = lax.broadcasted_iota(jnp.int32, (1, pix), 1)
    column = lax.rem(place, COLS)
    col_ok = {-1: column > 0, 1: column < COLS - 1}
    row_ok = {-1: place >= COLS, 1: place < pix - COLS}

    def unfold(value, store):
        for c in (-1, 0, 1):
            moved = value
            if c != 0:
                moved = jnp.where(col_ok[c], pltpu.roll(value, (-c) % pix, 1), 0.0)
            for r in (-1, 0, 1):
                out = moved
                if r != 0:
                    out = jnp.where(row_ok[r], pltpu.roll(moved, (-r * COLS) % pix, 1), 0.0)
                store(3 * (r + 1) + c + 1, out.astype(BF16))

    def unfold_y(value, t, plane):
        def store(w, out):
            base = plane * window + w * half
            cols[t, base : base + half, :] = out

        unfold(value.astype(F32), store)

    for t in range(frames):
        for z in range(planes):
            unfold_y(x_ref[t, z, 0:half, :], t, z + 1)

    @pl.when(has_l)
    def _():
        y_right.wait_recv()
        for t in range(frames):
            unfold_y(yh[0, t], t, 0)

    @pl.when(jnp.logical_not(has_l))
    def _():
        for t in range(frames):
            cols[t, 0:window, :] = jnp.zeros((window, pix), BF16)

    @pl.when(has_r)
    def _():
        y_left.wait_recv()
        for t in range(frames):
            unfold_y(yh[1, t], t, planes + 1)

    @pl.when(jnp.logical_not(has_r))
    def _():
        for t in range(frames):
            cols[t, (planes + 1) * window : (planes + 2) * window, :] = jnp.zeros((window, pix), BF16)

    whole = wcat[...]
    tw = tw_ref[...]
    for t in range(frames):
        for z in range(planes):
            pre = nn(whole, cols[t, z * window : (z + 3) * window, :]) + bias
            sig = jax.nn.sigmoid(pre)
            active = (pre * sig).astype(BF16)
            slope[t, z] = sig * (1.0 + pre * (1.0 - sig))
            act[t, z] = active
            mown[t, z] = nn(tw, active)
        if t == 0:
            for z in range(planes):
                msend[1, z] = mown[0, z, 2 * half : 3 * half, :].astype(BF16)
        if t == frames - 1:
            for z in range(planes):
                msend[0, z] = mown[t, z, 0:half, :].astype(BF16)
    m_right = remote(msend.at[0], mrecv.at[0], msem_s.at[0], msem_r.at[0], (me_g, ta_r))
    m_left = remote(msend.at[1], mrecv.at[1], msem_s.at[1], msem_r.at[1], (me_g, ta_l))
    m_right.start()

    ones = jnp.ones((8, pix), BF16)
    ssum = jnp.zeros((3 * window, hid), F32)
    tsum = jnp.zeros((3 * half, hid), F32)
    bsum = jnp.zeros((8, hid), F32)
    for z in range(planes):
        g_left[z].wait_recv()
        g_right[z].wait_recv()
        for t in range(frames):
            around = g3[t, z]
            hgrad = (tn(tw, around) * slope[t, z]).astype(BF16)
            hgr[t, z] = hgrad
            tsum = tsum + nt(around, act[t, z])
            bsum = bsum + nt(ones, hgrad)
            ssum = ssum + nt(cols[t, z * window : (z + 3) * window, :], hgrad)
    acc[0:window, 0:hid] = ssum[0:window]
    acc[0:window, hid : 2 * hid] = ssum[window : 2 * window]
    acc[window : 2 * window, 0:hid] = ssum[2 * window : 3 * window]
    used = window + 3 * half
    acc[window:used, hid : 2 * hid] = tsum
    acc[used : used + 8, hid : 2 * hid] = bsum
    acc[used + 8 : 2 * window, hid : 2 * hid] = jnp.zeros((2 * window - used - 8, hid), F32)
    if acc.shape[0] > 2 * window:
        acc[2 * window :, :] = jnp.zeros((acc.shape[0] - 2 * window, 2 * hid), F32)
    accb[...] = acc[...].astype(BF16)

    rows = acc.shape[0] // near_count

    def span(index):
        return pl.ds(pl.multiple_of(index * rows, 16), rows)

    near_me = member(near_bits, 0)[1]
    far_me = member(far_bits, 0)[1]
    scatter, share, gather = [], [], []
    for j in range(1, near_count):
        dev, index = member(near_bits, j)
        scatter.append(remote(accb.at[span(index)], first.at[j - 1], asem_s.at[j - 1], asem_r.at[j - 1], dev))
        mine = fin.at[span(near_me)]
        gather.append(remote(mine, mine, csem_s.at[j - 1], csem_r.at[j - 1], dev))
    for j in range(1, far_count):
        dev, _ = member(far_bits, j)
        share.append(remote(second.at[far_me], second.at[far_me], bsem_s.at[j - 1], bsem_r.at[j - 1], dev))
    for copy in scatter:
        copy.start()
    m_left.start()

    def step_share():
        total = acc[span(near_me), :]
        for j, copy in enumerate(scatter):
            copy.wait_recv()
            total = total + first[j].astype(F32)
        second[pl.ds(far_me, 1)] = total.astype(BF16)[None]
        for copy in share:
            copy.start()

    def step_gather():
        for copy in share:
            copy.wait_recv()
        total = second[0].astype(F32)
        for j in range(1, far_count):
            total = total + second[j].astype(F32)
        fin[span(near_me), :] = total.astype(BF16)
        for copy in gather:
            copy.start()

    back = flip[...]

    def p_right(t):
        return remote(psend.at[0, t], precv.at[0, t], psem_s.at[0, t], psem_r.at[0, t], (me_g + 1, me_t))

    def p_left(t):
        return remote(psend.at[1, t], precv.at[1, t], psem_s.at[1, t], psem_r.at[1, t], (me_g - 1, me_t))

    for t in range(frames):
        for z in range(planes):
            at = t * planes + z

            def store(w, out):
                hcols[at, w * hid : (w + 1) * hid, :] = out

            unfold(hgr[t, z].astype(F32), store)
            parts[t, z] = nn(back, hcols[at])
            if z == 0:
                psend[1, t] = parts[t, z, 0:half, :].astype(BF16)
                pl.when(has_l)(p_left(t).start)
            if z == planes - 1:
                psend[0, t] = parts[t, z, 2 * half : 3 * half, :].astype(BF16)
                pl.when(has_r)(p_right(t).start)
            if at == max(frames * planes - 2, 0):
                step_share()

    m_right.wait_recv()
    m_left.wait_recv()
    for t in range(frames):
        for z in range(planes):
            total = mown[t, z, half : 2 * half, :]
            total = total + (mown[t - 1, z, 0:half, :] if t > 0 else mrecv[0, z].astype(F32))
            total = total + (mown[t + 1, z, 2 * half : 3 * half, :] if t < frames - 1 else mrecv[1, z].astype(F32))
            rebuilt_ref[t, z] = (x_ref[t, z, half : 2 * half, :].astype(F32) - total).astype(BF16)
    step_gather()

    @pl.when(has_l)
    def _():
        for t in range(frames):
            p_right(t).wait_recv()

    @pl.when(jnp.logical_not(has_l))
    def _():
        precv[0] = jnp.zeros_like(precv[0])

    @pl.when(has_r)
    def _():
        for t in range(frames):
            p_left(t).wait_recv()

    @pl.when(jnp.logical_not(has_r))
    def _():
        precv[1] = jnp.zeros_like(precv[1])

    for t in range(frames):
        for z in range(planes):
            total = parts[t, z, half : 2 * half, :]
            total = total + (parts[t, z - 1, 2 * half : 3 * half, :] if z > 0 else precv[0, t].astype(F32))
            total = total + (parts[t, z + 1, 0:half, :] if z < planes - 1 else precv[1, t].astype(F32))
            gin_ref[t, z] = (g_ref[t, z, 0:half, :].astype(F32) + total).astype(BF16)

    for copy in gather:
        copy.wait_recv()

    pl.when(has_r)(y_right.wait_send)
    pl.when(has_l)(y_left.wait_send)
    for z in range(planes):
        g_left[z].wait_send()
        g_right[z].wait_send()
    m_right.wait_send()
    m_left.wait_send()

    @pl.when(has_r)
    def _():
        for t in range(frames):
            p_right(t).wait_send()

    @pl.when(has_l)
    def _():
        for t in range(frames):
            p_left(t).wait_send()

    for copy in scatter + share + gather:
        copy.wait_send()


def finish(factor, rebuilt_in, gin_in, fin, rebuilt_ref, gin_ref, gs_ref, gb_ref, gt_ref):
    hid, window = gs_ref.shape[1], gs_ref.shape[2]
    half = window // 9
    rebuilt_ref[...] = rebuilt_in[...]
    gin_ref[...] = gin_in[...]
    turned = (fin[0:window, :].astype(F32) * factor).T
    gs_ref[0] = turned[0:hid]
    gs_ref[1] = turned[hid : 2 * hid]
    low = fin[window : 2 * window, :].astype(F32) * factor
    gs_ref[2] = low.T[0:hid]
    for k in range(3):
        gt_ref[k] = low[k * half : (k + 1) * half, hid : 2 * hid]
    gb_ref[...] = low[3 * half : 3 * half + 1, hid : 2 * hid]


def shards(gz_count, ta_count, outputs_fwd, cotangent, spatial_weight, hidden_bias, temporal_weight):
    frames, planes, channels, pix = outputs_fwd.shape
    half = channels // 2
    hid = spatial_weight.shape[1]
    window = 9 * half
    tw = temporal_weight.reshape((3 * half, hid))
    factor = 1.0 / math.sqrt(frames * ta_count * planes * gz_count * ROWS * COLS)
    vmem = pl.BlockSpec(memory_space=pltpu.VMEM)
    near_bits, far_bits = groups_of(gz_count, ta_count)
    near_count, far_count = 1 << len(near_bits), 1 << len(far_bits)
    rows = slot_rows(window, near_count)
    dma = pltpu.SemaphoreType.DMA
    field = jax.ShapeDtypeStruct((frames, planes, half, pix), BF16)
    outs = pl.pallas_call(
        functools.partial(kernel, gz_count, ta_count),
        out_shape=(
            field,
            field,
            jax.ShapeDtypeStruct((near_count * rows, 2 * hid), BF16),
        ),
        in_specs=[pl.BlockSpec(memory_space=pltpu.HBM)] * 5,
        out_specs=(vmem,) * 3,
        scratch_shapes=[
            pltpu.VMEM((frames, (planes + 2) * window, pix), BF16),
            pltpu.VMEM((frames * planes, 9 * hid, pix), BF16),
            pltpu.VMEM((frames, planes, 3 * half, pix), BF16),
            pltpu.VMEM((2, frames, half, pix), BF16),
            pltpu.VMEM((frames, planes, hid, pix), F32),
            pltpu.VMEM((frames, planes, hid, pix), BF16),
            pltpu.VMEM((frames, planes, hid, pix), BF16),
            pltpu.VMEM((frames, planes, 3 * half, pix), F32),
            pltpu.VMEM((frames, planes, 3 * half, pix), F32),
            pltpu.VMEM((2, planes, half, pix), BF16),
            pltpu.VMEM((2, planes, half, pix), BF16),
            pltpu.VMEM((2, frames, half, pix), BF16),
            pltpu.VMEM((2, frames, half, pix), BF16),
            pltpu.VMEM(outputs_fwd.shape, BF16),
            pltpu.VMEM(cotangent.shape, BF16),
            pltpu.VMEM(spatial_weight.shape, BF16),
            pltpu.VMEM((1, hid), F32),
            pltpu.VMEM(tw.shape, BF16),
            dma((5,)),
            pltpu.VMEM((hid, 3 * window), BF16),
            pltpu.VMEM((3 * half, 9 * hid), BF16),
            pltpu.VMEM((near_count * rows, 2 * hid), F32),
            pltpu.VMEM((near_count * rows, 2 * hid), BF16),
            pltpu.VMEM((near_count - 1, rows, 2 * hid), BF16),
            pltpu.VMEM((far_count, rows, 2 * hid), BF16),
            dma((2,)), dma((2,)), dma((2, planes)), dma((2, planes)), dma((2,)), dma((2,)),
            dma((2, frames)), dma((2, frames)),
            dma((near_count - 1,)), dma((near_count - 1,)),
            dma((far_count - 1,)), dma((far_count - 1,)),
            dma((near_count - 1,)), dma((near_count - 1,)),
        ],
        compiler_params=pltpu.CompilerParams(
            collective_id=0, has_side_effects=True, vmem_limit_bytes=60 * 1024 * 1024
        ),
    )(outputs_fwd, cotangent, spatial_weight, hidden_bias[None, :], tw)
    ends = pl.pallas_call(
        functools.partial(finish, factor),
        out_shape=(
            field,
            field,
            jax.ShapeDtypeStruct((3, hid, window), F32),
            jax.ShapeDtypeStruct((1, hid), F32),
            jax.ShapeDtypeStruct((3, half, hid), F32),
        ),
        in_specs=[vmem] * 3,
        out_specs=(vmem,) * 5,
        compiler_params=pltpu.CompilerParams(vmem_limit_bytes=60 * 1024 * 1024),
    )(*outs)
    return ends[0], ends[1], ends[2], ends[3].reshape((hid,)), ends[4]


def solution(mesh):
    placed = (P("ta", "gz", None, None), P("ta", "gz", None, None), P(), P(), P())
    return jax.shard_map(
        functools.partial(shards, mesh.shape["gz"], mesh.shape["ta"]),
        mesh=mesh,
        in_specs=placed,
        out_specs=(P("ta", "gz", None, None), P("ta", "gz", None, None), P(), P(), P()),
        check_vma=False,
    )
```
